256 devices in a mesh: layer: 4 (over x), ex: 64 (over z, y, core).
Axes of the slice: x: 4, y: 4, z: 8, core: 2. Of those that a mesh axis runs over, the one named last changes fastest.
Arguments:
- query_factors: bfloat16 [4, 1024, 512, 128], P('layer', 'ex'), may hold values from -1.2578125 to 1.2578125
- response_lengths: int32 [1024], P('ex'), may hold values from 1 to 512, 262144 in all
- inverse_hessian: float32 [4, 4096, 4096], P('layer', 'ex'), as said below
- stored_gradients: bfloat16 [4, 16384, 4096], P('layer', 'ex'), may hold values from -0.015625 to 0.015625
Outputs:
- scores: float32 [1024, 16384], P('layer', 'ex')
The draws below stay inside these ranges and needn't reach their ends.
Inputs may be any that keep to these rules, and one draw needn't show every extreme that they name: inverse_hessian[l] is symmetric for every layer l.
All inputs are finite; a program needn't handle non-finite values. No bound on the sum of `response_lengths` on one device may be relied on, other than what follows from the above.
Results may differ from the reference program's by a relative error of at most 0.004.
Values may be sent and summed in bfloat16 or wider, within the bound.
No kernel may reach another device: no remote copies, remote signals or barrier semaphores. Data moves between devices by JAX's collectives and lax.ppermute only.
A program may use at most 64 MiB of HBM per device.

```python
import math
import jax
import jax.numpy as jnp
import numpy as np
from jax import lax

RANK = 64
DIM = 4096
MAXLEN = 512
LAYERS = 4
QUERIES = 1024
EXAMPLES = 16384


def draw_inverse_hessian(key, part):
    first_key, second_key = jax.random.split(jax.random.fold_in(key, 17))
    noise = jax.random.normal(first_key, (LAYERS, DIM, DIM), jnp.float32)
    diagonal = jax.random.uniform(second_key, (LAYERS, DIM), jnp.float32, 2.5, 4.5)
    spread = 0.7
    symmetric = (noise + jnp.swapaxes(noise, 1, 2)) * (spread / math.sqrt(2.0 * DIM))
    return symmetric + diagonal[:, :, None] * jnp.eye(DIM, dtype=jnp.float32)[None, :, :]


def block_levels(rng, extent, cuts, least, high):
    level, own = 1.0, jax.random.fold_in(rng, 6)
    for position, parts in cuts:
        steps = jnp.exp(jax.random.uniform(jax.random.fold_in(own, position), (parts,), jnp.float32, least / len(cuts), high / len(cuts)))
        level = level * jnp.repeat(steps, extent[position] // parts).reshape([-1 if axis == position else 1 for axis in range(len(extent))])
    return level


def profile(amount, total, limit, slope):
    loads = [(1 << 20) // math.isqrt(grade ** slope) + 1 for grade in range(2, amount + 1)]
    rest, holding = total - limit - (amount - 1), [1] * (amount - 1)
    while rest > 0:
        movable = [i for i in range(amount - 1) if holding[i] < limit]
        whole, remaining = sum([loads[i] for i in movable]), rest
        for i in movable:
            extra = min(limit - holding[i], max(1, remaining * loads[i] // whole), rest)
            holding[i] = holding[i] + extra
            rest = rest - extra
    return np.array([limit] + holding)


def ragged(rng, count, total, most, skew):
    if count == 2:
        one = jax.random.randint(rng, (), max(1, total - most), min(most, total - 1) + 1)
        return jnp.stack([one, total - one])
    tallies = jnp.asarray(profile(count, total, most, skew), jnp.int32)
    couples = (count - 1) // 2
    giver, sink = tallies[1:1 + 2 * couples:2], tallies[2:2 + 2 * couples:2]
    room = jnp.minimum(giver - 1, most - sink)
    passed = jax.random.randint(jax.random.fold_in(rng, 1), (couples,), 0, 1 << 20) % (room + 1)
    tallies = tallies.at[1:1 + 2 * couples:2].set(giver - passed).at[2:2 + 2 * couples:2].set(sink + passed)
    return tallies[jax.random.permutation(jax.random.fold_in(rng, 2), count)]


def centred(stream_key, dims, width, most, shards=(), held_as=jnp.bfloat16):
    loudness = block_levels(stream_key, dims, shards, -0.22, 0.18) if shards else 1.0
    drawn = jax.random.normal(stream_key, dims, jnp.float32) * width * loudness
    return jnp.minimum(jnp.maximum(drawn, -most), most).astype(held_as)


def setup_inputs(seed: int = 0) -> dict:
    seeds = jax.random.split(jax.random.key(seed), 5)
    query_factors = centred(seeds[0], (LAYERS, QUERIES, MAXLEN, 2 * RANK), (MAXLEN ** -0.25), 1.2578125, ((0, 4), (1, 64)))
    response_lengths = ragged(seeds[1], QUERIES, QUERIES * MAXLEN // 2, MAXLEN, 2).astype(jnp.int32)
    inverse_hessian = draw_inverse_hessian(jax.random.fold_in(seeds[4], 71), 0)
    stored_gradients = centred(seeds[3], (LAYERS, EXAMPLES, DIM), (9 * DIM * LAYERS) ** -0.5, 0.015625, ((0, 4), (1, 64)))
    return dict(query_factors=query_factors, response_lengths=response_lengths, inverse_hessian=inverse_hessian, stored_gradients=stored_gradients)


def layer_scores(query_layer, response_lengths, inverse_layer, stored_layer):
    steps = jnp.arange(MAXLEN, dtype=jnp.int32)
    mask = (steps[None, :] < response_lengths[:, None]).astype(jnp.bfloat16)
    inputs = query_layer[:, :, :RANK] * mask[:, :, None]
    outputs = query_layer[:, :, RANK:]
    projected = jnp.einsum("qti,qtj->qij", outputs.astype(jnp.float32), inputs.astype(jnp.float32))
    projected = projected.reshape(QUERIES, DIM).astype(jnp.bfloat16)
    preconditioned = jnp.dot(projected.astype(jnp.float32), inverse_layer, precision=lax.Precision.HIGHEST, preferred_element_type=jnp.float32).astype(jnp.bfloat16)
    return lax.dot_general(preconditioned, stored_layer, (((1,), (1,)), ((), ())), preferred_element_type=jnp.float32)


def reference(query_factors, response_lengths, inverse_hessian, stored_gradients):
    def one_layer(carry, items):
        query_layer, inverse_layer, stored_layer = items
        return carry + layer_scores(query_layer, response_lengths, inverse_layer, stored_layer), None

    start = jnp.zeros((QUERIES, EXAMPLES), jnp.float32)
    scores, unused = lax.scan(one_layer, start, (query_factors, inverse_hessian, stored_gradients))
    return scores
```

```python
import jax
import jax.numpy as jnp
from jax import lax
from jax.experimental import pallas as pl
from jax.experimental.pallas import tpu as pltpu
from jax.sharding import Mesh, PartitionSpec as P

LAYER, Z, Y, CORE = 4, 8, 4, 2
PIECES = Z * Y // 2
BF = jnp.bfloat16
F32 = jnp.float32
VMEM = pl.BlockSpec(memory_space=pltpu.VMEM)
SMEM = pl.BlockSpec(memory_space=pltpu.SMEM)
NT = (((1,), (1,)), ((), ()))
TN = (((0,), (0,)), ((), ()))


def params(mib=8):
    return pltpu.CompilerParams(vmem_limit_bytes=mib << 20)


def cost(flops, moved):
    return pl.CostEstimate(flops=flops // 1000, bytes_accessed=moved // 1000, transcendentals=0)


def gradient_kernel(lengths_ref, factors_ref, out_ref):
    queries, steps, width = factors_ref.shape
    rank = width // 2
    step = lax.broadcasted_iota(jnp.int32, (steps, width), 0)
    for q in range(queries):
        x = factors_ref[q]
        masked = jnp.where(step < lengths_ref[pl.program_id(0) * queries + q], x, jnp.zeros_like(x))
        both = lax.dot_general(x, masked, TN, preferred_element_type=F32)
        out_ref[q] = both[rank:, :rank].astype(BF)


def gradients(factors, lengths, group=4):
    queries, steps, width = factors.shape
    rank = width // 2
    projected = pl.pallas_call(
        gradient_kernel,
        out_shape=jax.ShapeDtypeStruct((queries, rank, rank), BF),
        grid_spec=pltpu.PrefetchScalarGridSpec(
            num_scalar_prefetch=1,
            grid=(queries // group,),
            in_specs=[pl.BlockSpec((group, steps, width), lambda i, _: (i, 0, 0))],
            out_specs=pl.BlockSpec((group, rank, rank), lambda i, _: (i, 0, 0)),
        ),
        compiler_params=params(6),
        cost_estimate=cost(queries * steps * width * width * 2, factors.size * 2),
        name="form_gradients",
    )(lengths, factors)
    return projected.reshape(queries, rank * rank)


def split_kernel(where_ref, own_ref, core_ref, chip_ref, both_ref, high_ref, low_ref):
    rows = own_ref.shape[0]
    me = where_ref[PIECES]
    for k, ref in enumerate((own_ref, core_ref, chip_ref, both_ref)):
        place = pl.ds(pl.multiple_of((me ^ k) * rows, rows), rows)
        whole = ref[...]
        high = whole.astype(BF)
        high_ref[place, :] = high
        low_ref[place, :] = (whole - high.astype(F32)).astype(BF)


def split_rows(where, parts):
    rows, columns = parts[0].shape
    shape = jax.ShapeDtypeStruct((4 * rows, columns), BF)
    return pl.pallas_call(
        split_kernel,
        out_shape=(shape, shape),
        in_specs=[SMEM] + [VMEM] * 4,
        out_specs=(VMEM, VMEM),
        compiler_params=params(16),
        cost_estimate=cost(rows * columns * 8, rows * columns * 32),
        name="split_inverse",
    )(where, *parts)


def precondition_kernel(count, where_ref, *refs):
    pieces, (high_ref, low_ref, out_ref) = refs[:count], refs[count:]
    rows = pieces[0].shape[0]
    left = jnp.concatenate([ref[...] for ref in pieces], axis=0)
    total = lax.dot_general(left, high_ref[...], NT, preferred_element_type=F32)
    total += lax.dot_general(left, low_ref[...], NT, preferred_element_type=F32)
    total = total.astype(BF)
    for k in range(count):
        place = pl.ds(pl.multiple_of(where_ref[k] * rows, rows), rows)
        out_ref[place, :] = total[k * rows : (k + 1) * rows]


def precondition(where, pieces, high, low):
    rows, depth = pieces[0].shape
    count = rows * len(pieces)
    return pl.pallas_call(
        lambda *refs: precondition_kernel(len(pieces), *refs),
        out_shape=jax.ShapeDtypeStruct((count, high.shape[0]), BF),
        in_specs=[SMEM] + [VMEM] * (len(pieces) + 2),
        out_specs=VMEM,
        compiler_params=params(16),
        cost_estimate=cost(4 * count * depth * high.shape[0], 2 * depth * (count + 2 * high.shape[0])),
        name="precondition",
    )(where, *pieces, high, low)


def score_kernel(some, held, first, cut, where_ref, *refs):
    count = len(some)
    pieces, stored, refs = refs[:count], refs[count : count + held], refs[count + held :]
    before, outs = (None, refs) if first else (refs[0], refs[1:])
    columns = pieces[0].shape[1]
    total = outs[-1] if cut else outs[0]
    start = 0
    for ref in stored:
        span = (slice(None), slice(start, start + ref.shape[0]))
        start += ref.shape[0]
        acc = None if first else before[span]
        for k, piece in enumerate(pieces):
            place = pl.ds(pl.multiple_of(where_ref[some[k]] * columns, columns), columns)
            term = lax.dot_general(piece[...], ref[:, place], NT, preferred_element_type=F32)
            acc = term if acc is None else acc + term
        total[span] = acc
    if cut:
        block = total.shape[0] // LAYER
        for k, out in enumerate(outs[:-1]):
            owner = lax.rem(where_ref[PIECES + 1] + k, LAYER)
            out[...] = total[pl.ds(pl.multiple_of(owner * block, block), block), :].astype(out.dtype)


def score(where, some, pieces, stored, before=None, cut=False):
    count = len(pieces)
    queries, columns = pieces[0].shape
    examples = sum(part.shape[0] for part in stored)
    whole = (queries, examples)
    block = (queries // LAYER, examples)
    depth = count * columns
    blocks = [jax.ShapeDtypeStruct(block, F32)] + [jax.ShapeDtypeStruct(block, BF)] * (LAYER - 1)
    more = [] if before is None else [before]
    return pl.pallas_call(
        lambda *refs: score_kernel(some, len(stored), before is None, cut, *refs),
        out_shape=blocks if cut else jax.ShapeDtypeStruct(whole, F32),
        in_specs=[SMEM] + [VMEM] * (count + len(stored) + len(more)),
        out_specs=[VMEM] * LAYER if cut else VMEM,
        scratch_shapes=[pltpu.VMEM(whole, F32)] if cut else [],
        compiler_params=params(20),
        cost_estimate=cost(2 * queries * depth * examples, 2 * depth * (queries + examples)),
        name="score",
    )(where, *pieces, *stored, *more)


def add_kernel(own_ref, a_ref, b_ref, c_ref, *outs):
    width = outs[0].shape[1]
    for k, out in enumerate(outs):
        part = (slice(None), slice(k * width, (k + 1) * width))
        out[...] = (own_ref[part] + a_ref[part].astype(F32)) + (b_ref[part].astype(F32) + c_ref[part].astype(F32))


def add_layers(own, others):
    rows, width = own.shape
    return pl.pallas_call(
        add_kernel,
        out_shape=[jax.ShapeDtypeStruct((rows, width // 4), F32)] * 4,
        in_specs=[VMEM] * 4,
        out_specs=[VMEM] * 4,
        compiler_params=params(6),
        cost_estimate=cost(rows * width * 3, rows * width * 14),
        name="add_layers",
    )(own, *others)


def place_kernel(where_ref, *refs):
    parts, out_ref = refs[:-1], refs[-1]
    rows = parts[0].shape[0] // 4
    for k, part in enumerate(parts):
        for group in range(4):
            start = pl.multiple_of(group * 4 * rows + (where_ref[PIECES] ^ k) * rows, rows)
            out_ref[pl.ds(start, rows), :] = part[group * rows : (group + 1) * rows, :]


def place_parts(where, parts):
    rows, width = parts[0].shape
    return pl.pallas_call(
        place_kernel,
        out_shape=jax.ShapeDtypeStruct((4 * rows, width), F32),
        in_specs=[SMEM] + [VMEM] * 4,
        out_specs=VMEM,
        compiler_params=params(6),
        cost_estimate=cost(rows * width * 4, rows * width * 32),
        name="place_parts",
    )(where, *parts)


def shift(value, axis, size, by):
    return lax.ppermute(value, axis, [(i, (i + by) % size) for i in range(size)])


def after(value, other):
    return lax.optimization_barrier((value, other))[0]


def swap_core(value):
    return lax.ppermute(value, "core", [(0, 1), (1, 0)])


def gather(own, across):
    pieces = []
    for side, value in enumerate((own, across)):
        pieces.append((0, side, value))
        up = down = value
        for distance in range(1, Z // 2):
            up = shift(up, "z", Z, 1)
            down = shift(down, "z", Z, -1)
            pieces.append((-distance, side, up))
            pieces.append((distance, side, down))
        last = shift(up, "z", Z, 1) if side == 0 else shift(down, "z", Z, -1)
        pieces.append((Z // 2, side, last))
    return pieces


def most(pieces):
    return [value for dz, side, value in pieces if abs(dz) + side == 3]


def per_device(factors, lengths, inverse, stored):
    layer, z, y, core = (lax.axis_index(name) for name in ("layer", "z", "y", "core"))
    apart = [distance for step in range(1, Z // 2) for distance in (-step, step)]
    apart = jnp.array([0] + apart + [Z // 2], jnp.int32)
    where = jnp.concatenate([((z + apart) % Z) * 2 + (y // 2 ^ side) for side in (0, 1)])
    where = jnp.concatenate([where, jnp.stack([(y % 2) * 2 + core, layer])]).astype(jnp.int32)
    inverse_rows, stored_rows = inverse[0], stored[0]

    def swap_chip(value, *pairs):
        return lax.ppermute(value, "y", [pair for a, b in pairs for pair in ((a, b), (b, a))])

    with jax.named_scope("swap_stored"):
        chip_stored = swap_chip(stored_rows, (0, 3), (1, 2))
    with jax.named_scope("gradients"):
        projected = gradients(factors[0], after(lengths, where))
    with jax.named_scope("gather_projected"):
        pieces = gather(projected, shift(projected, "y", Y, 2))
    with jax.named_scope("swap_inverse"):
        core_rows = swap_core(inverse_rows)
        chip_rows = swap_chip(after(inverse_rows, projected), (0, 1), (2, 3))
        both_rows = swap_core(after(chip_rows, most(pieces)))
    with jax.named_scope("split_inverse"):
        high, low = split_rows(where, (inverse_rows, core_rows, chip_rows, both_rows))
    with jax.named_scope("precondition"):
        own = precondition(where, [value for _, _, value in pieces], high, low)
    with jax.named_scope("gather_preconditioned"):
        pieces = gather(own, shift(own, "y", Y, 2))
    with jax.named_scope("swap_stored"):
        core_stored = swap_core(after(stored_rows, own))
        both_stored = swap_core(after(chip_stored, most(pieces)))
    with jax.named_scope("score"):
        late = [k for k, (dz, side, _) in enumerate(pieces) if abs(dz) == 4 or (side and abs(dz) == 3)]
        soon = [k for k in range(len(pieces)) if k not in late]
        stored_parts = (stored_rows, core_stored, chip_stored, both_stored)
        total = None
        for some in (soon, late):
            total = score(where, some, [pieces[k][2] for k in some], stored_parts, total, some is late)
        kept, *sent = total
    with jax.named_scope("sum_layers"):
        others = [shift(value, "layer", LAYER, k + 1) for k, value in enumerate(sent)]
        parts = add_layers(kept, others)
    with jax.named_scope("exchange_examples"):
        pairs = []
        for k in range(1, 4):
            pairs.append([(a * 2 + b, ((3 - a) if k & 2 else a) * 2 + (b ^ (k & 1))) for a in range(Y) for b in range(CORE)])
        parts = [parts[0]] + [lax.ppermute(parts[k], ("y", "core"), pairs[k - 1]) for k in range(1, 4)]
        return place_parts(where, parts)


def solution(mesh):
    shape = (LAYER, Z, Y, CORE)
    fine = Mesh(mesh.devices.reshape(shape), ("layer", "z", "y", "core"))
    ex = ("z", "y", "core")
    placed = (P("layer", ex, None, None), P(ex), P("layer", ex, None), P("layer", ex, None))
    return jax.shard_map(per_device, mesh=fine, in_specs=placed, out_specs=P("layer", ex), check_vma=False)
```

```python
import jax
import jax.numpy as jnp
from jax import lax
from jax.experimental import pallas as pl
from jax.experimental.pallas import tpu as pltpu
from jax.sharding import Mesh, PartitionSpec as P

LAYER, Z, Y, CORE = 4, 8, 4, 2
PIECES = Z * Y // 2
SELF = 3 * PIECES
BF = jnp.bfloat16
F32 = jnp.float32
VMEM = pl.BlockSpec(memory_space=pltpu.VMEM)
SMEM = pl.BlockSpec(memory_space=pltpu.SMEM)
NT = (((1,), (1,)), ((), ()))
TN = (((0,), (0,)), ((), ()))


def params(mib=8):
    return pltpu.CompilerParams(vmem_limit_bytes=mib << 20)


def cost(flops, moved):
    return pl.CostEstimate(flops=flops, bytes_accessed=moved, transcendentals=0)


def gradient_kernel(lengths_ref, factors_ref, out_ref):
    queries, steps, width = factors_ref.shape
    rank = width // 2
    step = lax.broadcasted_iota(jnp.int32, (steps, width), 0)
    for q in range(queries):
        x = factors_ref[q]
        masked = jnp.where(step < lengths_ref[pl.program_id(0) * queries + q], x, jnp.zeros_like(x))
        both = lax.dot_general(x, masked, TN, preferred_element_type=F32)
        out_ref[q] = both[rank:, :rank].astype(BF)


def gradients(factors, lengths, group=4):
    queries, steps, width = factors.shape
    rank = width // 2
    projected = pl.pallas_call(
        gradient_kernel,
        out_shape=jax.ShapeDtypeStruct((queries, rank, rank), BF),
        grid_spec=pltpu.PrefetchScalarGridSpec(
            num_scalar_prefetch=1,
            grid=(queries // group,),
            in_specs=[pl.BlockSpec((group, steps, width), lambda i, _: (i, 0, 0))],
            out_specs=pl.BlockSpec((group, rank, rank), lambda i, _: (i, 0, 0)),
        ),
        compiler_params=params(6),
        cost_estimate=cost(queries * steps * width * width * 2, factors.size * 2),
        name="form_gradients",
    )(lengths, factors)
    return projected.reshape(queries, rank * rank)


def split_kernel(where_ref, own_ref, core_ref, chip_ref, both_ref, high_ref, low_ref):
    rows = own_ref.shape[0]
    me = where_ref[SELF]
    for k, ref in enumerate((own_ref, core_ref, chip_ref, both_ref)):
        place = pl.ds(pl.multiple_of((me ^ k) * rows, rows), rows)
        whole = ref[...]
        high = whole.astype(BF)
        high_ref[place, :] = high
        low_ref[place, :] = (whole - high.astype(F32)).astype(BF)


def split_rows(where, parts):
    rows, columns = parts[0].shape
    shape = jax.ShapeDtypeStruct((4 * rows, columns), BF)
    return pl.pallas_call(
        split_kernel,
        out_shape=(shape, shape),
        in_specs=[SMEM] + [VMEM] * 4,
        out_specs=(VMEM, VMEM),
        compiler_params=params(16),
        cost_estimate=cost(rows * columns * 8, rows * columns * 32),
        name="split_inverse",
    )(where, *parts)


def precondition_kernel(count, where_ref, *refs):
    pieces, (high_ref, low_ref, out_ref) = refs[:count], refs[count:]
    rows = pieces[0].shape[0]
    left = jnp.concatenate([ref[...] for ref in pieces], axis=0)
    total = lax.dot_general(left, high_ref[...], NT, preferred_element_type=F32)
    total += lax.dot_general(left, low_ref[...], NT, preferred_element_type=F32)
    total = total.astype(BF)
    for k in range(count):
        place = pl.ds(pl.multiple_of(where_ref[k] * rows, rows), rows)
        out_ref[place, :] = total[k * rows : (k + 1) * rows]


def precondition(where, pieces, high, low):
    rows, depth = pieces[0].shape
    count = rows * len(pieces)
    return pl.pallas_call(
        lambda *refs: precondition_kernel(len(pieces), *refs),
        out_shape=jax.ShapeDtypeStruct((count, high.shape[0]), BF),
        in_specs=[SMEM] + [VMEM] * (len(pieces) + 2),
        out_specs=VMEM,
        compiler_params=params(16),
        cost_estimate=cost(4 * count * depth * high.shape[0], 2 * depth * (count + 2 * high.shape[0])),
        name="precondition",
    )(where, *pieces, high, low)


def score_kernel(some, held, first, cut, where_ref, *refs):
    count = len(some)
    pieces, stored, refs = refs[:count], refs[count : count + held], refs[count + held :]
    before, outs = (None, refs) if first else (refs[0], refs[1:])
    width = pieces[0].shape[1] // 2
    total = outs[-1] if cut else outs[0]
    examples = 0
    for ref in stored:
        span = (slice(None), slice(examples, examples + ref.shape[0]))
        examples += ref.shape[0]
        acc = None if first else before[span]
        for k, piece in enumerate(pieces):
            blocks = [
                ref[:, pl.ds(pl.multiple_of(where_ref[start + some[k]] * width, width), width)]
                for start in (PIECES, 2 * PIECES)
            ]
            right = jnp.concatenate(blocks, axis=1)
            term = lax.dot_general(piece[...], right, NT, preferred_element_type=F32)
            acc = term if acc is None else acc + term
        total[span] = acc
    if cut:
        block = total.shape[0] // LAYER
        for k, out in enumerate(outs[:-1]):
            owner = lax.rem(where_ref[SELF + 1] + k, LAYER)
            out[...] = total[pl.ds(pl.multiple_of(owner * block, block), block), :].astype(out.dtype)


def score(where, some, pieces, stored, before=None, cut=False):
    count = len(pieces)
    queries, columns = pieces[0].shape
    examples = sum(part.shape[0] for part in stored)
    whole = (queries, examples)
    block = (queries // LAYER, examples)
    depth = count * columns
    blocks = [jax.ShapeDtypeStruct(block, F32)] + [jax.ShapeDtypeStruct(block, BF)] * (LAYER - 1)
    more = [] if before is None else [before]
    return pl.pallas_call(
        lambda *refs: score_kernel(some, len(stored), before is None, cut, *refs),
        out_shape=blocks if cut else jax.ShapeDtypeStruct(whole, F32),
        in_specs=[SMEM] + [VMEM] * (count + len(stored) + len(more)),
        out_specs=[VMEM] * LAYER if cut else VMEM,
        scratch_shapes=[pltpu.VMEM(whole, F32)] if cut else [],
        compiler_params=params(20),
        cost_estimate=cost(2 * queries * depth * examples, 2 * depth * (queries + examples)),
        name="score",
    )(where, *pieces, *stored, *more)


def add_kernel(own_ref, a_ref, b_ref, c_ref, *outs):
    width = outs[0].shape[1]
    for k, out in enumerate(outs):
        part = (slice(None), slice(k * width, (k + 1) * width))
        total = (own_ref[part] + a_ref[part].astype(F32)) + (b_ref[part].astype(F32) + c_ref[part].astype(F32))
        out[...] = total.astype(out.dtype)


def add_layers(own, others):
    rows, width = own.shape
    return pl.pallas_call(
        add_kernel,
        out_shape=[jax.ShapeDtypeStruct((rows, width // 4), F32 if k == 0 else BF) for k in range(4)],
        in_specs=[VMEM] * 4,
        out_specs=[VMEM] * 4,
        compiler_params=params(6),
        cost_estimate=cost(rows * width * 3, rows * width * 14),
        name="add_layers",
    )(own, *others)


def place_kernel(where_ref, *refs):
    parts, out_ref = refs[:-1], refs[-1]
    rows = parts[0].shape[0] // 4
    for k, part in enumerate(parts):
        giver = where_ref[SELF] ^ k
        for group in range(4):
            start = (group // 2) * 8 + (group % 2) * 2 + lax.shift_right_logical(giver, 1) * 4 + (giver & 1)
            place = pl.ds(pl.multiple_of(start * rows, rows), rows)
            out_ref[place, :] = part[group * rows : (group + 1) * rows, :].astype(out_ref.dtype)


def place_parts(where, parts):
    rows, width = parts[0].shape
    return pl.pallas_call(
        place_kernel,
        out_shape=jax.ShapeDtypeStruct((4 * rows, width), F32),
        in_specs=[SMEM] + [VMEM] * 4,
        out_specs=VMEM,
        compiler_params=params(6),
        cost_estimate=cost(rows * width * 4, rows * width * 32),
        name="place_parts",
    )(where, *parts)


def shift(value, axis, size, by):
    return lax.ppermute(value, axis, [(i, (i + by) % size) for i in range(size)])


def after(value, other):
    return lax.optimization_barrier((value, other))[0]


def swap_core(value):
    return lax.ppermute(value, "core", [(0, 1), (1, 0)])


def gather(own, across):
    pieces = []
    for side, value in enumerate((own, across)):
        pieces.append((0, side, value))
        up = down = value
        for distance in range(1, Z // 2):
            up = shift(up, "z", Z, 1)
            down = shift(down, "z", Z, -1)
            pieces.append((-distance, side, up))
            pieces.append((distance, side, down))
        last = shift(up, "z", Z, 1) if side == 0 else shift(down, "z", Z, -1)
        pieces.append((Z // 2, side, last))
    return pieces


def some(pieces, *which):
    return [value for dz, side, value in pieces if (dz, side) in which]


def per_device(factors, lengths, inverse, stored):
    layer, z, y, core = (lax.axis_index(name) for name in ("layer", "z", "y", "core"))
    apart = [distance for step in range(1, Z // 2) for distance in (-step, step)]
    apart = jnp.array([0] + apart + [Z // 2], jnp.int32)
    depth, group = jnp.tile((z + apart) % Z, 2), y // 2
    parity = jnp.repeat(jnp.stack([y % 2, 1 - y % 2]), Z)
    first = parity ^ group
    where = jnp.concatenate(
        [depth * 2 + parity, depth * Y + first, depth * Y + Y - 1 - first, jnp.stack([group * 2 + core, layer])]
    ).astype(jnp.int32)
    inverse_rows, stored_rows = inverse[0], stored[0]

    def swap_chip(value, *pairs):
        return lax.ppermute(value, "y", [pair for a, b in pairs for pair in ((a, b), (b, a))])

    with jax.named_scope("gradients"):
        projected = gradients(factors[0], after(lengths, where))
    with jax.named_scope("gather_projected"):
        pieces = gather(projected, swap_chip(projected, (0, 1), (2, 3)))
    with jax.named_scope("swap_inverse"):
        core_rows = swap_core(inverse_rows)
        chip_rows = swap_chip(inverse_rows, (0, 3), (1, 2))
        both_rows = swap_core(after(chip_rows, some(pieces, (2, 0), (-2, 0), (2, 1), (-2, 1))))
    with jax.named_scope("swap_stored"):
        chip_stored = swap_chip(after(stored_rows, some(pieces, (1, 0), (-1, 0), (0, 1))), (0, 3), (1, 2))
    with jax.named_scope("split_inverse"):
        high, low = split_rows(where, (inverse_rows, core_rows, chip_rows, both_rows))
    with jax.named_scope("precondition"):
        own = precondition(where, [value for _, _, value in pieces], high, low)
    with jax.named_scope("gather_preconditioned"):
        pieces = gather(own, swap_chip(own, (0, 1), (2, 3)))
    with jax.named_scope("swap_stored"):
        core_stored = swap_core(after(stored_rows, own))
        both_stored = swap_core(after(chip_stored, some(pieces, (2, 0), (-2, 0), (2, 1), (-2, 1))))
    with jax.named_scope("score"):
        late = [k for k, (dz, side, _) in enumerate(pieces) if abs(dz) == 4 or (side and abs(dz) == 3)]
        soon = [k for k in range(len(pieces)) if k not in late]
        stored_parts = (stored_rows, core_stored, chip_stored, both_stored)
        total = None
        for part in (soon, late):
            total = score(where, part, [pieces[k][2] for k in part], stored_parts, total, part is late)
        kept, *sent = total
    with jax.named_scope("sum_layers"):
        others = [shift(value, "layer", LAYER, k + 1) for k, value in enumerate(sent)]
        parts = add_layers(kept, others)
    with jax.named_scope("exchange_examples"):
        pairs = []
        for k in range(1, 4):
            pairs.append([(a * 2 + b, ((3 - a) if k & 2 else a) * 2 + (b ^ (k & 1))) for a in range(Y) for b in range(CORE)])
        parts = [parts[0]] + [lax.ppermute(parts[k], ("y", "core"), pairs[k - 1]) for k in range(1, 4)]
        return place_parts(where, parts)


def solution(mesh):
    shape = (LAYER, Z, Y, CORE)
    fine = Mesh(mesh.devices.reshape(shape), ("layer", "z", "y", "core"))
    ex = ("z", "y", "core")
    placed = (P("layer", ex, None, None), P(ex), P("layer", ex, None), P("layer", ex, None))
    return jax.shard_map(per_device, mesh=fine, in_specs=placed, out_specs=P("layer", ex), check_vma=False)
```

```python
import jax
import jax.numpy as jnp
from jax import lax
from jax.experimental import pallas as pl
from jax.experimental.pallas import tpu as pltpu
from jax.sharding import Mesh, PartitionSpec as P

LAYER, Z, Y, CORE = 4, 8, 4, 2
PIECES = Z * Y // 2
SELF = 3 * PIECES
BF = jnp.bfloat16
F32 = jnp.float32
VMEM = pl.BlockSpec(memory_space=pltpu.VMEM)
SMEM = pl.BlockSpec(memory_space=pltpu.SMEM)
NT = (((1,), (1,)), ((), ()))
TN = (((0,), (0,)), ((), ()))


def params(mib=8):
    return pltpu.CompilerParams(vmem_limit_bytes=mib << 20)


def cost(flops, moved):
    return pl.CostEstimate(flops=flops, bytes_accessed=moved, transcendentals=0)


def gradient_kernel(lengths_ref, factors_ref, out_ref):
    queries, steps, width = factors_ref.shape
    rank = width // 2
    step = lax.broadcasted_iota(jnp.int32, (steps, width), 0)
    for q in range(queries):
        x = factors_ref[q]
        masked = jnp.where(step < lengths_ref[pl.program_id(0) * queries + q], x, jnp.zeros_like(x))
        both = lax.dot_general(x, masked, TN, preferred_element_type=F32)
        out_ref[q] = both[rank:, :rank].astype(BF)


def gradients(factors, lengths, group=4):
    queries, steps, width = factors.shape
    rank = width // 2
    projected = pl.pallas_call(
        gradient_kernel,
        out_shape=jax.ShapeDtypeStruct((queries, rank, rank), BF),
        grid_spec=pltpu.PrefetchScalarGridSpec(
            num_scalar_prefetch=1,
            grid=(queries // group,),
            in_specs=[pl.BlockSpec((group, steps, width), lambda i, _: (i, 0, 0))],
            out_specs=pl.BlockSpec((group, rank, rank), lambda i, _: (i, 0, 0)),
        ),
        compiler_params=params(6),
        cost_estimate=cost(queries * steps * width * width * 2, factors.size * 2),
        name="form_gradients",
    )(lengths, factors)
    return projected.reshape(queries, rank * rank)


def split_kernel(where_ref, own_ref, core_ref, chip_ref, both_ref, high_ref, low_ref):
    rows = own_ref.shape[0]
    me = where_ref[SELF]
    for k, ref in enumerate((own_ref, core_ref, chip_ref, both_ref)):
        place = pl.ds(pl.multiple_of((me ^ k) * rows, rows), rows)
        whole = ref[...]
        high = whole.astype(BF)
        high_ref[place, :] = high
        low_ref[place, :] = (whole - high.astype(F32)).astype(BF)


def split_rows(where, parts):
    rows, columns = parts[0].shape
    shape = jax.ShapeDtypeStruct((4 * rows, columns), BF)
    return pl.pallas_call(
        split_kernel,
        out_shape=(shape, shape),
        in_specs=[SMEM] + [VMEM] * 4,
        out_specs=(VMEM, VMEM),
        compiler_params=params(16),
        cost_estimate=cost(rows * columns * 8, rows * columns * 32),
        name="split_inverse",
    )(where, *parts)


def precondition_kernel(count, where_ref, *refs):
    pieces, (high_ref, low_ref, out_ref) = refs[:count], refs[count:]
    rows = pieces[0].shape[0]
    left = jnp.concatenate([ref[...] for ref in pieces], axis=0)
    total = lax.dot_general(left, high_ref[...], NT, preferred_element_type=F32)
    total += lax.dot_general(left, low_ref[...], NT, preferred_element_type=F32)
    total = total.astype(BF)
    for k in range(count):
        place = pl.ds(pl.multiple_of(where_ref[k] * rows, rows), rows)
        out_ref[place, :] = total[k * rows : (k + 1) * rows]


def precondition(where, pieces, high, low):
    rows, depth = pieces[0].shape
    count = rows * len(pieces)
    return pl.pallas_call(
        lambda *refs: precondition_kernel(len(pieces), *refs),
        out_shape=jax.ShapeDtypeStruct((count, high.shape[0]), BF),
        in_specs=[SMEM] + [VMEM] * (len(pieces) + 2),
        out_specs=VMEM,
        compiler_params=params(16),
        cost_estimate=cost(4 * count * depth * high.shape[0], 2 * depth * (count + 2 * high.shape[0])),
        name="precondition",
    )(where, *pieces, high, low)


def score_kernel(some, held, first, cut, where_ref, *refs):
    count = len(some)
    pieces, stored, refs = refs[:count], refs[count : count + held], refs[count + held :]
    before, outs = (None, refs) if first else (refs[0], refs[1:])
    width = pieces[0].shape[1] // 2
    total = outs[-1] if cut else outs[0]
    examples = 0
    for ref in stored:
        span = (slice(None), slice(examples, examples + ref.shape[0]))
        examples += ref.shape[0]
        acc = None if first else before[span]
        for k, piece in enumerate(pieces):
            blocks = [
                ref[:, pl.ds(pl.multiple_of(where_ref[start + some[k]] * width, width), width)]
                for start in (PIECES, 2 * PIECES)
            ]
            right = jnp.concatenate(blocks, axis=1)
            term = lax.dot_general(piece[...], right, NT, preferred_element_type=F32)
            acc = term if acc is None else acc + term
        total[span] = acc
    if cut:
        block = total.shape[0] // LAYER
        for k, out in enumerate(outs[:-1]):
            owner = lax.rem(where_ref[SELF + 1] + k, LAYER)
            out[...] = total[pl.ds(pl.multiple_of(owner * block, block), block), :].astype(out.dtype)


def score(where, some, pieces, stored, before=None, cut=False):
    count = len(pieces)
    queries, columns = pieces[0].shape
    examples = sum(part.shape[0] for part in stored)
    whole = (queries, examples)
    block = (queries // LAYER, examples)
    depth = count * columns
    blocks = [jax.ShapeDtypeStruct(block, F32)] + [jax.ShapeDtypeStruct(block, BF)] * (LAYER - 1)
    more = [] if before is None else [before]
    return pl.pallas_call(
        lambda *refs: score_kernel(some, len(stored), before is None, cut, *refs),
        out_shape=blocks if cut else jax.ShapeDtypeStruct(whole, F32),
        in_specs=[SMEM] + [VMEM] * (count + len(stored) + len(more)),
        out_specs=[VMEM] * LAYER if cut else VMEM,
        scratch_shapes=[pltpu.VMEM(whole, F32)] if cut else [],
        compiler_params=params(20),
        cost_estimate=cost(2 * queries * depth * examples, 2 * depth * (queries + examples)),
        name="score",
    )(where, *pieces, *stored, *more)


def add_kernel(own_ref, a_ref, b_ref, c_ref, *outs):
    width = outs[0].shape[1]
    for k, out in enumerate(outs):
        part = (slice(None), slice(k * width, (k + 1) * width))
        total = (own_ref[part] + a_ref[part].astype(F32)) + (b_ref[part].astype(F32) + c_ref[part].astype(F32))
        out[...] = total.astype(out.dtype)


def add_layers(own, others):
    rows, width = own.shape
    return pl.pallas_call(
        add_kernel,
        out_shape=[jax.ShapeDtypeStruct((rows, width // 4), F32 if k == 0 else BF) for k in range(4)],
        in_specs=[VMEM] * 4,
        out_specs=[VMEM] * 4,
        compiler_params=params(6),
        cost_estimate=cost(rows * width * 3, rows * width * 14),
        name="add_layers",
    )(own, *others)


def place_kernel(where_ref, *refs):
    parts, out_ref = refs[:-1], refs[-1]
    rows = parts[0].shape[0] // 4
    for k, part in enumerate(parts):
        giver = where_ref[SELF] ^ k
        for group in range(4):
            start = (group // 2) * 8 + (group % 2) * 2 + lax.shift_right_logical(giver, 1) * 4 + (giver & 1)
            place = pl.ds(pl.multiple_of(start * rows, rows), rows)
            out_ref[place, :] = part[group * rows : (group + 1) * rows, :].astype(out_ref.dtype)


def place_parts(where, parts):
    rows, width = parts[0].shape
    return pl.pallas_call(
        place_kernel,
        out_shape=jax.ShapeDtypeStruct((4 * rows, width), F32),
        in_specs=[SMEM] + [VMEM] * 4,
        out_specs=VMEM,
        compiler_params=params(6),
        cost_estimate=cost(rows * width * 4, rows * width * 32),
        name="place_parts",
    )(where, *parts)


def shift(value, axis, size, by):
    return lax.ppermute(value, axis, [(i, (i + by) % size) for i in range(size)])


def after(value, other):
    return lax.optimization_barrier((value, other))[0]


def swap_core(value):
    return lax.ppermute(value, "core", [(0, 1), (1, 0)])


def gather(own, across):
    pieces = []
    for side, value in enumerate((own, across)):
        pieces.append((0, side, value))
        up = down = value
        for distance in range(1, Z // 2):
            up = shift(up, "z", Z, 1)
            down = shift(down, "z", Z, -1)
            pieces.append((-distance, side, up))
            pieces.append((distance, side, down))
        last = shift(up, "z", Z, 1) if side == 0 else shift(down, "z", Z, -1)
        pieces.append((Z // 2, side, last))
    return pieces


def some(pieces, *which):
    return [value for dz, side, value in pieces if (dz, side) in which]


def per_device(factors, lengths, inverse, stored):
    layer, z, y, core = (lax.axis_index(name) for name in ("layer", "z", "y", "core"))
    apart = [distance for step in range(1, Z // 2) for distance in (-step, step)]
    apart = jnp.array([0] + apart + [Z // 2], jnp.int32)
    depth, group = jnp.tile((z + apart) % Z, 2), y // 2
    parity = jnp.repeat(jnp.stack([y % 2, 1 - y % 2]), Z)
    first = parity ^ group
    where = jnp.concatenate(
        [depth * 2 + parity, depth * Y + first, depth * Y + Y - 1 - first, jnp.stack([group * 2 + core, layer])]
    ).astype(jnp.int32)
    inverse_rows, stored_rows = inverse[0], stored[0]

    def swap_chip(value, *pairs):
        return lax.ppermute(value, "y", [pair for a, b in pairs for pair in ((a, b), (b, a))])

    with jax.named_scope("gradients"):
        projected = gradients(factors[0], after(lengths, where))
    with jax.named_scope("gather_projected"):
        pieces = gather(projected, swap_chip(projected, (0, 1), (2, 3)))
    with jax.named_scope("swap_inverse"):
        core_rows = swap_core(inverse_rows)
        chip_rows = swap_chip(inverse_rows, (0, 3), (1, 2))
        both_rows = swap_core(after(chip_rows, some(pieces, (2, 0), (-2, 0), (2, 1), (-2, 1))))
    with jax.named_scope("swap_stored"):
        chip_stored = swap_chip(after(stored_rows, some(pieces, (1, 0), (-1, 0), (0, 1))), (0, 3), (1, 2))
    with jax.named_scope("split_inverse"):
        high, low = split_rows(where, (inverse_rows, core_rows, chip_rows, both_rows))
    with jax.named_scope("precondition"):
        own = precondition(where, [value for _, _, value in pieces], high, low)
    with jax.named_scope("gather_preconditioned"):
        pieces = gather(own, swap_chip(own, (0, 1), (2, 3)))
    with jax.named_scope("swap_stored"):
        core_stored = swap_core(after(stored_rows, own))
        both_stored = swap_core(after(chip_stored, some(pieces, (3, 0), (-3, 0), (3, 1), (-3, 1))))
    with jax.named_scope("score"):
        late = [k for k, (dz, side, _) in enumerate(pieces) if abs(dz) == 4 or (side and abs(dz) == 3)]
        soon = [k for k in range(len(pieces)) if k not in late]
        stored_parts = (stored_rows, core_stored, chip_stored, both_stored)
        total = None
        for part in (soon, late):
            total = score(where, part, [pieces[k][2] for k in part], stored_parts, total, part is late)
        kept, *sent = total
    with jax.named_scope("sum_layers"):
        others = [shift(value, "layer", LAYER, k + 1) for k, value in enumerate(sent)]
        parts = add_layers(kept, others)
    with jax.named_scope("exchange_examples"):
        pairs = []
        for k in range(1, 4):
            pairs.append([(a * 2 + b, ((3 - a) if k & 2 else a) * 2 + (b ^ (k & 1))) for a in range(Y) for b in range(CORE)])
        parts = [parts[0]] + [lax.ppermute(parts[k], ("y", "core"), pairs[k - 1]) for k in range(1, 4)]
        return place_parts(where, parts)


def solution(mesh):
    shape = (LAYER, Z, Y, CORE)
    fine = Mesh(mesh.devices.reshape(shape), ("layer", "z", "y", "core"))
    ex = ("z", "y", "core")
    placed = (P("layer", ex, None, None), P(ex), P("layer", ex, None), P("layer", ex, None))
    return jax.shard_map(per_device, mesh=fine, in_specs=placed, out_specs=P("layer", ex), check_vma=False)
```

```python
import jax
import jax.numpy as jnp
from jax import lax
from jax.experimental import pallas as pl
from jax.experimental.pallas import tpu as pltpu
from jax.sharding import Mesh, PartitionSpec as P

LAYER, Z, Y, CORE = 4, 8, 4, 2
PIECES = Z * Y // 2
SELF = 3 * PIECES
BF = jnp.bfloat16
F32 = jnp.float32
VMEM = pl.BlockSpec(memory_space=pltpu.VMEM)
SMEM = pl.BlockSpec(memory_space=pltpu.SMEM)
NT = (((1,), (1,)), ((), ()))
TN = (((0,), (0,)), ((), ()))


def params(mib=8):
    return pltpu.CompilerParams(vmem_limit_bytes=mib << 20)


def cost(flops, moved):
    return pl.CostEstimate(flops=flops, bytes_accessed=moved, transcendentals=0)


def gradient_kernel(lengths_ref, factors_ref, out_ref):
    queries, steps, width = factors_ref.shape
    rank = width // 2
    step = lax.broadcasted_iota(jnp.int32, (steps, width), 0)
    for q in range(queries):
        x = factors_ref[q]
        masked = jnp.where(step < lengths_ref[pl.program_id(0) * queries + q], x, jnp.zeros_like(x))
        both = lax.dot_general(x, masked, TN, preferred_element_type=F32)
        out_ref[q] = both[rank:, :rank].astype(BF)


def gradients(factors, lengths, group=4):
    queries, steps, width = factors.shape
    rank = width // 2
    projected = pl.pallas_call(
        gradient_kernel,
        out_shape=jax.ShapeDtypeStruct((queries, rank, rank), BF),
        grid_spec=pltpu.PrefetchScalarGridSpec(
            num_scalar_prefetch=1,
            grid=(queries // group,),
            in_specs=[pl.BlockSpec((group, steps, width), lambda i, _: (i, 0, 0))],
            out_specs=pl.BlockSpec((group, rank, rank), lambda i, _: (i, 0, 0)),
        ),
        compiler_params=params(6),
        cost_estimate=cost(queries * steps * width * width * 2, factors.size * 2),
        name="form_gradients",
    )(lengths, factors)
    return projected.reshape(queries, rank * rank)


def split_kernel(where_ref, own_ref, core_ref, chip_ref, both_ref, high_ref, low_ref):
    rows = own_ref.shape[0]
    me = where_ref[SELF]
    for k, ref in enumerate((own_ref, core_ref, chip_ref, both_ref)):
        place = pl.ds(pl.multiple_of((me ^ k) * rows, rows), rows)
        whole = ref[...]
        high = whole.astype(BF)
        high_ref[place, :] = high
        low_ref[place, :] = (whole - high.astype(F32)).astype(BF)


def split_rows(where, parts):
    rows, columns = parts[0].shape
    shape = jax.ShapeDtypeStruct((4 * rows, columns), BF)
    return pl.pallas_call(
        split_kernel,
        out_shape=(shape, shape),
        in_specs=[SMEM] + [VMEM] * 4,
        out_specs=(VMEM, VMEM),
        compiler_params=params(16),
        cost_estimate=cost(rows * columns * 8, rows * columns * 32),
        name="split_inverse",
    )(where, *parts)


def precondition_kernel(count, where_ref, *refs):
    pieces, (high_ref, low_ref, out_ref) = refs[:count], refs[count:]
    rows = pieces[0].shape[0]
    left = jnp.concatenate([ref[...] for ref in pieces], axis=0)
    total = lax.dot_general(left, high_ref[...], NT, preferred_element_type=F32)
    total += lax.dot_general(left, low_ref[...], NT, preferred_element_type=F32)
    total = total.astype(BF)
    for k in range(count):
        place = pl.ds(pl.multiple_of(where_ref[k] * rows, rows), rows)
        out_ref[place, :] = total[k * rows : (k + 1) * rows]


def precondition(where, pieces, high, low):
    rows, depth = pieces[0].shape
    count = rows * len(pieces)
    return pl.pallas_call(
        lambda *refs: precondition_kernel(len(pieces), *refs),
        out_shape=jax.ShapeDtypeStruct((count, high.shape[0]), BF),
        in_specs=[SMEM] + [VMEM] * (len(pieces) + 2),
        out_specs=VMEM,
        compiler_params=params(16),
        cost_estimate=cost(4 * count * depth * high.shape[0], 2 * depth * (count + 2 * high.shape[0])),
        name="precondition",
    )(where, *pieces, high, low)


def score_kernel(some, held, first, cut, where_ref, *refs):
    count = len(some)
    pieces, stored, refs = refs[:count], refs[count : count + held], refs[count + held :]
    before, outs = (None, refs) if first else (refs[0], refs[1:])
    width = pieces[0].shape[1] // 2
    total = outs[-1] if cut else outs[0]
    examples = 0
    for ref in stored:
        span = (slice(None), slice(examples, examples + ref.shape[0]))
        examples += ref.shape[0]
        acc = None if first else before[span]
        for k, piece in enumerate(pieces):
            blocks = [
                ref[:, pl.ds(pl.multiple_of(where_ref[start + some[k]] * width, width), width)]
                for start in (PIECES, 2 * PIECES)
            ]
            right = jnp.concatenate(blocks, axis=1)
            term = lax.dot_general(piece[...], right, NT, preferred_element_type=F32)
            acc = term if acc is None else acc + term
        total[span] = acc
    if cut:
        block = total.shape[0] // LAYER
        for k, out in enumerate(outs[:-1]):
            owner = lax.rem(where_ref[SELF + 1] + k, LAYER)
            out[...] = total[pl.ds(pl.multiple_of(owner * block, block), block), :].astype(out.dtype)


def score(where, some, pieces, stored, before=None, cut=False):
    count = len(pieces)
    queries, columns = pieces[0].shape
    examples = sum(part.shape[0] for part in stored)
    whole = (queries, examples)
    block = (queries // LAYER, examples)
    depth = count * columns
    blocks = [jax.ShapeDtypeStruct(block, F32)] + [jax.ShapeDtypeStruct(block, BF)] * (LAYER - 1)
    more = [] if before is None else [before]
    return pl.pallas_call(
        lambda *refs: score_kernel(some, len(stored), before is None, cut, *refs),
        out_shape=blocks if cut else jax.ShapeDtypeStruct(whole, F32),
        in_specs=[SMEM] + [VMEM] * (count + len(stored) + len(more)),
        out_specs=[VMEM] * LAYER if cut else VMEM,
        scratch_shapes=[pltpu.VMEM(whole, F32)] if cut else [],
        compiler_params=params(20),
        cost_estimate=cost(2 * queries * depth * examples, 2 * depth * (queries + examples)),
        name="score",
    )(where, *pieces, *stored, *more)


def add_kernel(own_ref, a_ref, b_ref, c_ref, *outs):
    width = outs[0].shape[1]
    for k, out in enumerate(outs):
        part = (slice(None), slice(k * width, (k + 1) * width))
        total = (own_ref[part] + a_ref[part].astype(F32)) + (b_ref[part].astype(F32) + c_ref[part].astype(F32))
        out[...] = total.astype(out.dtype)


def add_layers(own, others):
    rows, width = own.shape
    return pl.pallas_call(
        add_kernel,
        out_shape=[jax.ShapeDtypeStruct((rows, width // 4), F32 if k == 0 else BF) for k in range(4)],
        in_specs=[VMEM] * 4,
        out_specs=[VMEM] * 4,
        compiler_params=params(6),
        cost_estimate=cost(rows * width * 3, rows * width * 14),
        name="add_layers",
    )(own, *others)


def place_kernel(where_ref, *refs):
    parts, out_ref = refs[:-1], refs[-1]
    rows = parts[0].shape[0] // 4
    for k, part in enumerate(parts):
        giver = where_ref[SELF] ^ k
        for group in range(4):
            start = (group // 2) * 8 + (group % 2) * 2 + lax.shift_right_logical(giver, 1) * 4 + (giver & 1)
            place = pl.ds(pl.multiple_of(start * rows, rows), rows)
            out_ref[place, :] = part[group * rows : (group + 1) * rows, :].astype(out_ref.dtype)


def place_parts(where, parts):
    rows, width = parts[0].shape
    return pl.pallas_call(
        place_kernel,
        out_shape=jax.ShapeDtypeStruct((4 * rows, width), F32),
        in_specs=[SMEM] + [VMEM] * 4,
        out_specs=VMEM,
        compiler_params=params(6),
        cost_estimate=cost(rows * width * 4, rows * width * 32),
        name="place_parts",
    )(where, *parts)


def shift(value, axis, size, by):
    return lax.ppermute(value, axis, [(i, (i + by) % size) for i in range(size)])


def after(value, other):
    return lax.optimization_barrier((value, other))[0]


def swap_core(value):
    return lax.ppermute(value, "core", [(0, 1), (1, 0)])


def gather(own, across):
    pieces = []
    for side, value in enumerate((own, across)):
        pieces.append((0, side, value))
        up = down = value
        for distance in range(1, Z // 2):
            up = shift(up, "z", Z, 1)
            down = shift(down, "z", Z, -1)
            pieces.append((-distance, side, up))
            pieces.append((distance, side, down))
        last = shift(up, "z", Z, 1) if side == 0 else shift(down, "z", Z, -1)
        pieces.append((Z // 2, side, last))
    return pieces


def some(pieces, *which):
    return [value for dz, side, value in pieces if (dz, side) in which]


def per_device(factors, lengths, inverse, stored):
    layer, z, y, core = (lax.axis_index(name) for name in ("layer", "z", "y", "core"))
    apart = [distance for step in range(1, Z // 2) for distance in (-step, step)]
    apart = jnp.array([0] + apart + [Z // 2], jnp.int32)
    depth, group = jnp.tile((z + apart) % Z, 2), y // 2
    parity = jnp.repeat(jnp.stack([y % 2, 1 - y % 2]), Z)
    first = parity ^ group
    where = jnp.concatenate(
        [depth * 2 + parity, depth * Y + first, depth * Y + Y - 1 - first, jnp.stack([group * 2 + core, layer])]
    ).astype(jnp.int32)
    inverse_rows, stored_rows = inverse[0], stored[0]

    def swap_chip(value, *pairs):
        return lax.ppermute(value, "y", [pair for a, b in pairs for pair in ((a, b), (b, a))])

    with jax.named_scope("gradients"):
        projected = gradients(factors[0], after(lengths, where))
    with jax.named_scope("gather_projected"):
        pieces = gather(projected, swap_chip(projected, (0, 1), (2, 3)))
    with jax.named_scope("swap_inverse"):
        core_rows = swap_core(inverse_rows)
        chip_rows = swap_chip(inverse_rows, (0, 3), (1, 2))
        both_rows = swap_core(after(chip_rows, some(pieces, (3, 0), (-3, 0), (3, 1), (-3, 1))))
    with jax.named_scope("swap_stored"):
        chip_stored = swap_chip(after(stored_rows, some(pieces, (1, 0), (-1, 0), (0, 1))), (0, 3), (1, 2))
    with jax.named_scope("split_inverse"):
        high, low = split_rows(where, (inverse_rows, core_rows, chip_rows, both_rows))
    with jax.named_scope("precondition"):
        own = precondition(where, [value for _, _, value in pieces], high, low)
    with jax.named_scope("gather_preconditioned"):
        pieces = gather(own, swap_chip(own, (0, 1), (2, 3)))
    with jax.named_scope("swap_stored"):
        core_stored = swap_core(after(stored_rows, own))
        both_stored = swap_core(after(chip_stored, some(pieces, (3, 0), (-3, 0), (3, 1), (-3, 1))))
    with jax.named_scope("score"):
        late = [k for k, (dz, side, _) in enumerate(pieces) if abs(dz) == 4 or (side and abs(dz) == 3)]
        soon = [k for k in range(len(pieces)) if k not in late]
        stored_parts = (stored_rows, core_stored, chip_stored, both_stored)
        total = None
        for part in (soon, late):
            total = score(where, part, [pieces[k][2] for k in part], stored_parts, total, part is late)
        kept, *sent = total
    with jax.named_scope("sum_layers"):
        others = [shift(value, "layer", LAYER, k + 1) for k, value in enumerate(sent)]
        parts = add_layers(kept, others)
    with jax.named_scope("exchange_examples"):
        pairs = []
        for k in range(1, 4):
            pairs.append([(a * 2 + b, ((3 - a) if k & 2 else a) * 2 + (b ^ (k & 1))) for a in range(Y) for b in range(CORE)])
        parts = [parts[0]] + [lax.ppermute(parts[k], ("y", "core"), pairs[k - 1]) for k in range(1, 4)]
        return place_parts(where, parts)


def solution(mesh):
    shape = (LAYER, Z, Y, CORE)
    fine = Mesh(mesh.devices.reshape(shape), ("layer", "z", "y", "core"))
    ex = ("z", "y", "core")
    placed = (P("layer", ex, None, None), P(ex), P("layer", ex, None), P("layer", ex, None))
    return jax.shard_map(per_device, mesh=fine, in_specs=placed, out_specs=P("layer", ex), check_vma=False)
```

```python
import jax
import jax.numpy as jnp
from jax import lax
from jax.experimental import pallas as pl
from jax.experimental.pallas import tpu as pltpu
from jax.sharding import Mesh, PartitionSpec as P

LAYER, Z, Y, CORE = 4, 8, 4, 2
PIECES = Z * Y // 2
SELF = 3 * PIECES
BF = jnp.bfloat16
F32 = jnp.float32
VMEM = pl.BlockSpec(memory_space=pltpu.VMEM)
SMEM = pl.BlockSpec(memory_space=pltpu.SMEM)
NT = (((1,), (1,)), ((), ()))
TN = (((0,), (0,)), ((), ()))


def params(mib=8):
    return pltpu.CompilerParams(vmem_limit_bytes=mib << 20)


def cost(flops, moved):
    return pl.CostEstimate(flops=flops, bytes_accessed=moved, transcendentals=0)


def gradient_kernel(lengths_ref, factors_ref, out_ref):
    queries, steps, width = factors_ref.shape
    rank = width // 2
    step = lax.broadcasted_iota(jnp.int32, (steps, width), 0)
    for q in range(queries):
        x = factors_ref[q]
        masked = jnp.where(step < lengths_ref[pl.program_id(0) * queries + q], x, jnp.zeros_like(x))
        both = lax.dot_general(x, masked, TN, preferred_element_type=F32)
        out_ref[q] = both[rank:, :rank].astype(BF)


def gradients(factors, lengths, group=4):
    queries, steps, width = factors.shape
    rank = width // 2
    projected = pl.pallas_call(
        gradient_kernel,
        out_shape=jax.ShapeDtypeStruct((queries, rank, rank), BF),
        grid_spec=pltpu.PrefetchScalarGridSpec(
            num_scalar_prefetch=1,
            grid=(queries // group,),
            in_specs=[pl.BlockSpec((group, steps, width), lambda i, _: (i, 0, 0))],
            out_specs=pl.BlockSpec((group, rank, rank), lambda i, _: (i, 0, 0)),
        ),
        compiler_params=params(6),
        cost_estimate=cost(queries * steps * width * width * 2, factors.size * 2),
        name="form_gradients",
    )(lengths, factors)
    return projected.reshape(queries, rank * rank)


def split_kernel(where_ref, own_ref, core_ref, chip_ref, both_ref, high_ref, low_ref):
    rows = own_ref.shape[0]
    me = where_ref[SELF]
    for k, ref in enumerate((own_ref, core_ref, chip_ref, both_ref)):
        place = pl.ds(pl.multiple_of((me ^ k) * rows, rows), rows)
        whole = ref[...]
        high = whole.astype(BF)
        high_ref[place, :] = high
        low_ref[place, :] = (whole - high.astype(F32)).astype(BF)


def split_rows(where, parts):
    rows, columns = parts[0].shape
    shape = jax.ShapeDtypeStruct((4 * rows, columns), BF)
    return pl.pallas_call(
        split_kernel,
        out_shape=(shape, shape),
        in_specs=[SMEM] + [VMEM] * 4,
        out_specs=(VMEM, VMEM),
        compiler_params=params(16),
        cost_estimate=cost(rows * columns * 8, rows * columns * 32),
        name="split_inverse",
    )(where, *parts)


def precondition_kernel(count, where_ref, *refs):
    pieces, (high_ref, low_ref, out_ref) = refs[:count], refs[count:]
    rows = pieces[0].shape[0]
    left = jnp.concatenate([ref[...] for ref in pieces], axis=0)
    total = lax.dot_general(left, high_ref[...], NT, preferred_element_type=F32)
    total += lax.dot_general(left, low_ref[...], NT, preferred_element_type=F32)
    total = total.astype(BF)
    for k in range(count):
        place = pl.ds(pl.multiple_of(where_ref[k] * rows, rows), rows)
        out_ref[place, :] = total[k * rows : (k + 1) * rows]


def precondition(where, pieces, high, low):
    rows, depth = pieces[0].shape
    count = rows * len(pieces)
    return pl.pallas_call(
        lambda *refs: precondition_kernel(len(pieces), *refs),
        out_shape=jax.ShapeDtypeStruct((count, high.shape[0]), BF),
        in_specs=[SMEM] + [VMEM] * (len(pieces) + 2),
        out_specs=VMEM,
        compiler_params=params(16),
        cost_estimate=cost(4 * count * depth * high.shape[0], 2 * depth * (count + 2 * high.shape[0])),
        name="precondition",
    )(where, *pieces, high, low)


def score_kernel(some, held, first, cut, where_ref, *refs):
    count = len(some)
    pieces, stored, refs = refs[:count], refs[count : count + held], refs[count + held :]
    before, outs = (None, refs) if first else (refs[0], refs[1:])
    width = pieces[0].shape[1] // 2
    total = outs[-1] if cut else outs[0]
    examples = 0
    for ref in stored:
        span = (slice(None), slice(examples, examples + ref.shape[0]))
        examples += ref.shape[0]
        acc = None if first else before[span]
        for k, piece in enumerate(pieces):
            blocks = [
                ref[:, pl.ds(pl.multiple_of(where_ref[start + some[k]] * width, width), width)]
                for start in (PIECES, 2 * PIECES)
            ]
            right = jnp.concatenate(blocks, axis=1)
            term = lax.dot_general(piece[...], right, NT, preferred_element_type=F32)
            acc = term if acc is None else acc + term
        total[span] = acc
    if cut:
        block = total.shape[0] // LAYER
        for k, out in enumerate(outs[:-1]):
            owner = lax.rem(where_ref[SELF + 1] + k, LAYER)
            out[...] = total[pl.ds(pl.multiple_of(owner * block, block), block), :].astype(out.dtype)


def score(where, some, pieces, stored, before=None, cut=False):
    count = len(pieces)
    queries, columns = pieces[0].shape
    examples = sum(part.shape[0] for part in stored)
    whole = (queries, examples)
    block = (queries // LAYER, examples)
    depth = count * columns
    blocks = [jax.ShapeDtypeStruct(block, F32)] + [jax.ShapeDtypeStruct(block, BF)] * (LAYER - 1)
    more = [] if before is None else [before]
    return pl.pallas_call(
        lambda *refs: score_kernel(some, len(stored), before is None, cut, *refs),
        out_shape=blocks if cut else jax.ShapeDtypeStruct(whole, F32),
        in_specs=[SMEM] + [VMEM] * (count + len(stored) + len(more)),
        out_specs=[VMEM] * LAYER if cut else VMEM,
        scratch_shapes=[pltpu.VMEM(whole, F32)] if cut else [],
        compiler_params=params(20),
        cost_estimate=cost(2 * queries * depth * examples, 2 * depth * (queries + examples)),
        name="score",
    )(where, *pieces, *stored, *more)


def add_kernel(own_ref, a_ref, b_ref, c_ref, *outs):
    width = outs[0].shape[1]
    for k, out in enumerate(outs):
        part = (slice(None), slice(k * width, (k + 1) * width))
        total = (own_ref[part] + a_ref[part].astype(F32)) + (b_ref[part].astype(F32) + c_ref[part].astype(F32))
        out[...] = total.astype(out.dtype)


def add_layers(own, others):
    rows, width = own.shape
    return pl.pallas_call(
        add_kernel,
        out_shape=[jax.ShapeDtypeStruct((rows, width // 4), F32 if k == 0 else BF) for k in range(4)],
        in_specs=[VMEM] * 4,
        out_specs=[VMEM] * 4,
        compiler_params=params(6),
        cost_estimate=cost(rows * width * 3, rows * width * 14),
        name="add_layers",
    )(own, *others)


def place_kernel(where_ref, *refs):
    parts, out_ref = refs[:-1], refs[-1]
    rows = parts[0].shape[0] // 4
    for k, part in enumerate(parts):
        giver = where_ref[SELF] ^ k
        for group in range(4):
            start = (group // 2) * 8 + (group % 2) * 2 + lax.shift_right_logical(giver, 1) * 4 + (giver & 1)
            place = pl.ds(pl.multiple_of(start * rows, rows), rows)
            out_ref[place, :] = part[group * rows : (group + 1) * rows, :].astype(out_ref.dtype)


def place_parts(where, parts):
    rows, width = parts[0].shape
    return pl.pallas_call(
        place_kernel,
        out_shape=jax.ShapeDtypeStruct((4 * rows, width), F32),
        in_specs=[SMEM] + [VMEM] * 4,
        out_specs=VMEM,
        compiler_params=params(6),
        cost_estimate=cost(rows * width * 4, rows * width * 32),
        name="place_parts",
    )(where, *parts)


def shift(value, axis, size, by):
    return lax.ppermute(value, axis, [(i, (i + by) % size) for i in range(size)])


def after(value, other):
    return lax.optimization_barrier((value, other))[0]


def swap_core(value):
    return lax.ppermute(value, "core", [(0, 1), (1, 0)])


def gather(own, across):
    pieces = []
    for side, value in enumerate((own, across)):
        pieces.append((0, side, value))
        up = down = value
        for distance in range(1, Z // 2):
            up = shift(up, "z", Z, 1)
            down = shift(down, "z", Z, -1)
            pieces.append((-distance, side, up))
            pieces.append((distance, side, down))
        last = shift(up, "z", Z, 1) if side == 0 else shift(down, "z", Z, -1)
        pieces.append((Z // 2, side, last))
    return pieces


def some(pieces, *which):
    return [value for dz, side, value in pieces if (dz, side) in which]


def per_device(factors, lengths, inverse, stored):
    layer, z, y, core = (lax.axis_index(name) for name in ("layer", "z", "y", "core"))
    apart = [distance for step in range(1, Z // 2) for distance in (-step, step)]
    apart = jnp.array([0] + apart + [Z // 2], jnp.int32)
    depth, group = jnp.tile((z + apart) % Z, 2), y // 2
    parity = jnp.repeat(jnp.stack([y % 2, 1 - y % 2]), Z)
    first = parity ^ group
    where = jnp.concatenate(
        [depth * 2 + parity, depth * Y + first, depth * Y + Y - 1 - first, jnp.stack([group * 2 + core, layer])]
    ).astype(jnp.int32)
    inverse_rows, stored_rows = inverse[0], stored[0]

    def swap_chip(value, *pairs):
        return lax.ppermute(value, "y", [pair for a, b in pairs for pair in ((a, b), (b, a))])

    with jax.named_scope("gradients"):
        projected = gradients(factors[0], after(lengths, where))
    with jax.named_scope("gather_projected"):
        pieces = gather(projected, swap_chip(projected, (0, 1), (2, 3)))
    with jax.named_scope("swap_inverse"):
        core_rows = swap_core(inverse_rows)
        chip_rows = swap_chip(inverse_rows, (0, 3), (1, 2))
        both_rows = swap_core(after(chip_rows, some(pieces, (3, 0), (-3, 0), (3, 1), (-3, 1))))
    with jax.named_scope("swap_stored"):
        chip_stored = swap_chip(after(stored_rows, some(pieces, (1, 0), (-1, 0), (0, 1))), (0, 3), (1, 2))
    with jax.named_scope("split_inverse"):
        high, low = split_rows(where, (inverse_rows, core_rows, chip_rows, both_rows))
    with jax.named_scope("precondition"):
        own = precondition(where, [value for _, _, value in pieces], high, low)
    with jax.named_scope("gather_preconditioned"):
        pieces = gather(own, swap_chip(own, (0, 1), (2, 3)))
    with jax.named_scope("swap_stored"):
        core_stored = swap_core(after(stored_rows, own))
        both_stored = swap_core(after(chip_stored, some(pieces, (3, 0), (-3, 0), (3, 1), (-3, 1))))
    with jax.named_scope("score"):
        late = [k for k, (dz, side, _) in enumerate(pieces) if abs(dz) == 4 or (side and abs(dz) == 3)]
        soon = [k for k in range(len(pieces)) if k not in late]
        stored_parts = (stored_rows, core_stored, chip_stored, both_stored)
        total = None
        for part in (soon, late):
            total = score(where, part, [pieces[k][2] for k in part], stored_parts, total, part is late)
        kept, *sent = total
    with jax.named_scope("sum_layers"):
        others = [shift(sent[k], "layer", LAYER, k + 1) for k in (1, 0, 2)]
        parts = add_layers(kept, others)
    with jax.named_scope("exchange_examples"):
        pairs = []
        for k in range(1, 4):
            pairs.append([(a * 2 + b, ((3 - a) if k & 2 else a) * 2 + (b ^ (k & 1))) for a in range(Y) for b in range(CORE)])
        parts = [parts[0]] + [lax.ppermute(parts[k], ("y", "core"), pairs[k - 1]) for k in range(1, 4)]
        return place_parts(where, parts)


def solution(mesh):
    shape = (LAYER, Z, Y, CORE)
    fine = Mesh(mesh.devices.reshape(shape), ("layer", "z", "y", "core"))
    ex = ("z", "y", "core")
    placed = (P("layer", ex, None, None), P(ex), P("layer", ex, None), P("layer", ex, None))
    return jax.shard_map(per_device, mesh=fine, in_specs=placed, out_specs=P("layer", ex), check_vma=False)
```
